1024 devices in a mesh: rows: 128 (over x, y, z_lo), aux: 8 (over z_hi, core).
Axes of the slice: x: 4, y: 8, z: 16 (z_hi: 4, z_lo: 4; z = z_hi * 4 + z_lo), core: 2. Of those that a mesh axis runs over, the one named last changes fastest.
Arguments:
- pair_green_block: bfloat16 [65536, 2048], P('rows', 'aux'), may hold values from -6 to 6
- cholesky_factors: bfloat16 [65536, 512], P('rows', 'aux'), may hold values from -0.09375 to 0.09375
- green_one: float32 [256, 256], replicated, may hold values from -0.375 to 0.375
- screening: float32 [512], replicated, may hold values from 0.25 to 4
Outputs:
- section_slope: float32 [65536, 2048], P('rows', 'aux')
- collision: float32 [65536], P(('rows', 'aux'))
The draws below stay inside these ranges and needn't reach their ends.
All inputs are finite; a program needn't handle non-finite values.
Results may differ from the reference program's by a relative error of at most 0.0029.
Values may be sent and summed in bfloat16 or wider, within the bound.
A program may use at most 32 MiB of HBM per device.

```python
import math
import jax
import jax.numpy as jnp
from jax import lax

NORB = 256
NAUX = 512
KSLAB = 8
PAIRS = 65536
SLAB = 2048


def level_of(stream_key, dims, split, low, largest):
    gain, own = 1.0, jax.random.fold_in(stream_key, 6)
    for dim, shards_of in split:
        draws = jnp.exp(jax.random.uniform(jax.random.fold_in(own, dim), (shards_of,), jnp.float32, low / len(split), largest / len(split)))
        gain = gain * jnp.repeat(draws, dims[dim] // shards_of).reshape([-1 if axis == dim else 1 for axis in range(len(dims))])
    return gain


def normal_values(own_key, extent, scale, most, cuts=(), kind=jnp.bfloat16):
    result = scale * jax.random.normal(own_key, extent, jnp.float32)
    if cuts:
        result = result * level_of(own_key, extent, cuts, -0.22, 0.18)
    return jnp.clip(result, -most, most).astype(kind)


def setup_inputs(seed: int = 0) -> dict:
    splits = jax.random.split(jax.random.key(seed), 5)
    pair_green_block = normal_values(splits[0], (PAIRS, SLAB), 1.0, 6.0, ((0, 128), (1, 8)))
    cholesky_factors = normal_values(splits[1], (PAIRS, NAUX), (NORB * NAUX // 32) ** -0.5, 0.09375, ((0, 128), (1, 8)))
    green_one = normal_values(splits[2], (NORB, NORB), NORB ** -0.5, 0.375, (), jnp.float32)
    screening = jnp.clip(jnp.exp(jax.random.uniform(splits[3], (NAUX,), jnp.float32, math.log(0.25), math.log(4.0))), 0.25, 4.0)
    return dict(pair_green_block=pair_green_block, cholesky_factors=cholesky_factors, green_one=green_one, screening=screening)


def reference(pair_green_block, cholesky_factors, green_one, screening):
    highest = lax.Precision.HIGHEST
    projected = lax.dot_general(cholesky_factors, pair_green_block, (((0,), (0,)), ((), ())), preferred_element_type=jnp.float32)
    shaped = projected.reshape(NAUX, KSLAB, NORB)
    dressed = jnp.einsum("qkm,ml->qkl", shaped, green_one, precision=highest)
    dressed = (dressed * screening[:, None, None]).reshape(NAUX, KSLAB * NORB).astype(jnp.bfloat16)
    section_slope = jnp.dot(cholesky_factors, dressed, preferred_element_type=jnp.float32)
    trace_weights = green_one[:, :KSLAB].T.reshape(KSLAB * NORB)
    collision = jnp.dot(section_slope, trace_weights, precision=highest, preferred_element_type=jnp.float32)
    return section_slope, collision
```

```python
import jax
import jax.numpy as jnp
from jax import lax
from jax.experimental import pallas as pl
from jax.experimental.pallas import tpu as pltpu
from jax.sharding import PartitionSpec as P

NX, NY, NZ, NH = 4, 8, 4, 4
F32, BF16 = jnp.float32, jnp.bfloat16
HIGHEST = lax.Precision.HIGHEST
NT = (((1,), (1,)), ((), ()))
NN = (((1,), (0,)), ((), ()))


def dot(a, b, dims=NN, precision=None):
    return lax.dot_general(a, b, dims, precision=precision, preferred_element_type=F32)


def iota(shape, axis):
    return lax.broadcasted_iota(jnp.int32, shape, axis)


def kernel(
    green_block, own_chol, green_one, screening, slope, collision,
    chol_t, part, part_in, ysum, y_in, z_all, dressed, chol_p, vec, vx, vy, vz, vh, vc,
    pc_send, pc_recv, z_send, z_recv, f_send, f_recv, x_send, x_recv, y_send, y_recv,
    l_send, l_recv, gy_send, gy_recv, gx_send, gx_recv,
    vx_send, vx_recv, vy_send, vy_recv, vz_send, vz_recv, vh_send, vh_recv, vc_send, vc_recv,
):
    row, aux = lax.axis_index("rows"), lax.axis_index("aux")
    mx, my, mz = row // (NY * NZ), (row // NZ) % NY, row % NZ
    mh, core = aux // 2, aux % 2

    def at_x(j):
        return {"rows": (((mx + j) % NX) * NY + my) * NZ + mz, "aux": aux}

    def at_y(j):
        return {"rows": (mx * NY + (my + j) % NY) * NZ + mz, "aux": aux}

    def at_z(j):
        return {"rows": (mx * NY + my) * NZ + (mz + j) % NZ, "aux": aux}

    def at_h(j):
        return {"rows": row, "aux": ((mh + j) % NH) * 2 + core}

    mate = {"rows": row, "aux": mh * 2 + 1 - core}
    sent = []

    def copy(src, dst, send, recv, to):
        made = pltpu.make_async_remote_copy(
            src_ref=src, dst_ref=dst, send_sem=send, recv_sem=recv,
            device_id=to, device_id_type=pl.DeviceIdType.MESH,
        )
        return made

    def send(*what):
        made = copy(*what)
        made.start()
        sent.append(made)

    chol_t[0, core] = own_chol[...]
    barrier = pltpu.get_barrier_semaphore()
    peers = [mate] + [at_x(j) for j in range(1, NX)] + [at_y(j) for j in range(1, NY)]
    peers += [at_z(j) for j in range(1, NZ)] + [at_h(j) for j in range(1, NH)]
    for peer in peers:
        pl.semaphore_signal(barrier, inc=1, device_id=peer, device_id_type=pl.DeviceIdType.MESH)
    pl.semaphore_wait(barrier, len(peers))

    half = 32
    for i in range(2):
        rows_i = pl.ds(i * half, half)
        for slot, step in ((1, 1), (2, -1)):
            send(own_chol.at[rows_i], chol_t.at[slot, core, rows_i], z_send.at[slot, i], z_recv.at[slot, i], at_h(step))
    send(own_chol, chol_t.at[0, core], pc_send.at[0, 0], pc_recv.at[0, 0], mate)

    def z_block(slot, i):
        rows_i = pl.ds(i * half, half)
        here = chol_t.at[slot, core, rows_i]
        return here, z_recv.at[slot, i]

    def await_z(slot, i):
        here, sem = z_block(slot, i)
        copy(here, here, z_send.at[slot, i], sem, mate).wait_recv()

    def to_mate(slot, i):
        here, _ = z_block(slot, i)
        send(here, here, pc_send.at[slot, i], pc_recv.at[slot, i], mate)

    def from_mate(slot, i):
        there = chol_t.at[slot, 1 - core, pl.ds(i * half, half)]
        copy(there, there, pc_send.at[slot, i], pc_recv.at[slot, i], mate).wait_recv()

    pick = (iota((8, 256), 1) == aux).astype(F32)
    column = dot(pick, green_one[...], NT, HIGHEST)
    trace_row = dot(column, green_one[...], NT, HIGHEST)

    slot_h = [mh, (mh + NH - 1) % NH, (mh + 1) % NH, (mh + 2) % NH]
    top = iota((8, 128), 0) < 4
    lane, sub = iota((8, 128), 1), iota((8, 128), 0)
    own_first = 4 * (mx * NY + my)
    scales = []
    for t in range(4):
        weights = jnp.broadcast_to(screening[pl.ds(slot_h[t], 1), :], (8, 128))
        scales.append(jnp.sum(jnp.where(lane == own_first + sub % 4, weights, 0.0), axis=1, keepdims=True))

    vec[...] = jnp.zeros((8, 128), F32)

    def project(t):
        block = dot(chol_t[t].reshape(128, 512), green_block[...])
        for j in range(16):
            left, right = block[8 * j : 8 * j + 8, :128], block[8 * j : 8 * j + 8, 128:]
            for e in range(2):
                g = 2 * j + e
                if e == 0:
                    tile = jnp.where(top, left, pltpu.roll(right, 4, 0))
                else:
                    tile = jnp.where(top, pltpu.roll(left, 4, 0), right)
                part[t, g // NY, g % NY] = tile
        for j in range(1, NX):
            send(part.at[t, (mx + j) % NX], part_in.at[t, j], x_send.at[t, j], x_recv.at[t, j], at_x(j))
        terms = dot(trace_row, block, NT, HIGHEST)
        vec[...] = jnp.where(sub == slot_h[t], terms, vec[...])

    def sum_x(t):
        total = part[t, mx]
        for j in range(1, NX):
            copy(part_in.at[t, j], part_in.at[t, j], x_send.at[t, j], x_recv.at[t, j], mate).wait_recv()
            total = total + part_in[t, j]
        ysum[t] = total
        for j in range(1, NY):
            send(ysum.at[t, (my + j) % NY], y_in.at[t, j], y_send.at[t, j], y_recv.at[t, j], at_y(j))

    def sum_y(t):
        total = ysum[t, my]
        for j in range(1, NY):
            copy(y_in.at[t, j], y_in.at[t, j], y_send.at[t, j], y_recv.at[t, j], mate).wait_recv()
            total = total + y_in[t, j]
        z_all[mz, t] = total
        for j in range(1, NZ):
            send(z_all.at[mz, t], z_all.at[mz, t], l_send.at[t, j], l_recv.at[t, j], at_z(j))

    def spread(value, store, sems, count, to):
        store[0] = value
        for j in range(1, count):
            send(store.at[0], store.at[j], sems[0].at[j], sems[1].at[j], to(j))

    def collect(store, sems, count):
        total = store[0]
        for j in range(1, count):
            copy(store.at[j], store.at[j], sems[0].at[j], sems[1].at[j], mate).wait_recv()
            total = total + store[j]
        return total

    from_mate_0 = chol_t.at[0, 1 - core]
    copy(from_mate_0, from_mate_0, pc_send.at[0, 0], pc_recv.at[0, 0], mate).wait_recv()
    project(0)

    far, near = 1 + core, 2 - core
    for i in range(2):
        await_z(far, i)
        here, _ = z_block(far, i)
        onward = {"rows": row, "aux": ((mh + 1 + 2 * core) % NH) * 2 + core}
        send(here, chol_t.at[3, core, pl.ds(i * half, half)], f_send.at[i], z_recv.at[3, i], onward)
        to_mate(far, i)
        await_z(near, i)
        to_mate(near, i)
    sum_x(0)
    for slot in (1, 2):
        for i in range(2):
            from_mate(slot, i)
        project(slot)
    for i in range(2):
        await_z(3, i)
        to_mate(3, i)
    for i in range(2):
        from_mate(3, i)
    project(3)
    sems_vx, sems_vy, sems_vz, sems_vh = (vx_send, vx_recv), (vy_send, vy_recv), (vz_send, vz_recv), (vh_send, vh_recv)
    spread(vec[...], vx, sems_vx, NX, at_x)
    sum_y(0)
    sum_x(1)
    sum_x(2)

    for b in range(4):
        new = iota((128, 512), 0) + 128 * b
        old = ((new >> 2) & 3) * 128 + (new >> 7) * 32 + ((new >> 4) & 7) * 4 + (new & 3)
        move = jnp.where(iota((128, 512), 1) == old, 1.0, 0.0).astype(BF16)
        moved = dot(move, chol_t[...].reshape(512, 512))
        chol_p[:, 128 * b : 128 * b + 128] = moved.T.astype(BF16)

    sum_x(3)
    spread(collect(vx, sems_vx, NX), vy, sems_vy, NY, at_y)
    sum_y(1)
    sum_y(2)
    sum_y(3)
    spread(collect(vy, sems_vy, NY), vz, sems_vz, NZ, at_z)

    for t in range(4):
        for j in range(1, NZ):
            there = z_all.at[(mz + NZ - j) % NZ, t]
            copy(there, there, l_send.at[t, j], l_recv.at[t, j], mate).wait_recv()
    total = (z_all[0] + z_all[1]) + (z_all[2] + z_all[3])
    flat = total.reshape(32, 128)
    upper = dot(flat, green_one[:128, :], NN, HIGHEST)
    lower = dot(flat, green_one[128:, :], NN, HIGHEST)
    done = []
    for t in range(4):
        both = upper[8 * t : 8 * t + 8] + pltpu.roll(lower[8 * t : 8 * t + 8], 4, 0)
        done.append(both * scales[t])
    top2 = iota((8, 256), 0) < 4
    first = jnp.where(top2, done[0], pltpu.roll(done[1], 4, 0))
    second = jnp.where(top2, done[2], pltpu.roll(done[3], 4, 0))
    dressed[mx, my] = jnp.concatenate([first, second], axis=0).astype(BF16)

    for j in range(1, NY):
        here = dressed.at[mx, my]
        send(here, here, gy_send.at[j], gy_recv.at[j], at_y(j))
    spread(collect(vz, sems_vz, NZ), vh, sems_vh, NH, at_h)
    for j in range(1, NY):
        there = dressed.at[mx, (my + NY - j) % NY]
        copy(there, there, gy_send.at[j], gy_recv.at[j], mate).wait_recv()
    for j in range(1, NX):
        here = dressed.at[mx]
        send(here, here, gx_send.at[j], gx_recv.at[j], at_x(j))
    for j in range(1, NX):
        there = dressed.at[(mx + NX - j) % NX]
        copy(there, there, gx_send.at[j], gx_recv.at[j], mate).wait_recv()
    vc[0] = collect(vh, sems_vh, NH)
    send(vc.at[0], vc.at[1], vc_send, vc_recv, mate)

    slope[...] = dot(chol_p[...], dressed[...].reshape(512, 256))

    copy(vc.at[1], vc.at[1], vc_send, vc_recv, mate).wait_recv()
    vec[...] = vc[0] + vc[1]
    traced = jnp.zeros((8, 512), F32)
    for t in range(4):
        weights = vec[pl.ds(slot_h[t], 1), :] * screening[pl.ds(slot_h[t], 1), :]
        weights = jnp.broadcast_to(weights, (8, 128))
        traced = traced + dot(weights, chol_t[t].reshape(128, 512).astype(F32), NN, HIGHEST)
    for a in range(2 * NH):
        @pl.when(aux == a)
        def _():
            collision[...] = traced[0:1, 64 * a : 64 * a + 64]

    for made in sent:
        made.wait_send()


def local(pair_green_block, cholesky_factors, green_one, screening):
    vmem, dma = pltpu.VMEM, pltpu.SemaphoreType.DMA
    slope, collision = pl.pallas_call(
        kernel,
        out_shape=(jax.ShapeDtypeStruct((512, 256), F32), jax.ShapeDtypeStruct((1, 64), F32)),
        in_specs=[pl.BlockSpec(memory_space=vmem)] * 4,
        out_specs=(pl.BlockSpec(memory_space=vmem), pl.BlockSpec(memory_space=vmem)),
        scratch_shapes=[
            vmem((4, 2, 64, 512), BF16),
            vmem((4, NX, NY, 8, 128), F32),
            vmem((4, NX, NY, 8, 128), F32),
            vmem((4, NY, 8, 128), F32),
            vmem((4, NY, 8, 128), F32),
            vmem((NZ, 4, 8, 128), F32),
            vmem((NX, NY, 16, 256), BF16),
            vmem((512, 512), BF16),
            vmem((8, 128), F32),
            vmem((NX, 8, 128), F32),
            vmem((NY, 8, 128), F32),
            vmem((NZ, 8, 128), F32),
            vmem((NH, 8, 128), F32),
            vmem((2, 8, 128), F32),
            dma((4, 2)), dma((4, 2)), dma((4, 2)), dma((4, 2)), dma((2,)), dma((2,)),
            dma((4, NX)), dma((4, NX)), dma((4, NY)), dma((4, NY)),
            dma((4, NZ)), dma((4, NZ)), dma((NY,)), dma((NY,)), dma((NX,)), dma((NX,)),
            dma((NX,)), dma((NX,)), dma((NY,)), dma((NY,)), dma((NZ,)), dma((NZ,)),
            dma((NH,)), dma((NH,)), dma, dma,
        ],
        compiler_params=pltpu.CompilerParams(collective_id=0, has_side_effects=True),
    )(pair_green_block, cholesky_factors.T, green_one, screening.reshape(4, 128))
    return slope, collision.reshape(64)


def solution(mesh):
    placed = (P("rows", "aux"), P("rows", "aux"), P(), P())
    return jax.shard_map(
        local,
        mesh=mesh,
        in_specs=placed,
        out_specs=(P("rows", "aux"), P(("rows", "aux"))),
        check_vma=False,
    )
```

```python
import jax
import jax.numpy as jnp
from jax import lax
from jax.experimental import pallas as pl
from jax.experimental.pallas import tpu as pltpu
from jax.sharding import PartitionSpec as P

NX, NY, NZ, NH = 4, 8, 4, 4
CHUNKS = 4
F32, BF16 = jnp.float32, jnp.bfloat16
HIGHEST = lax.Precision.HIGHEST
MESH = pl.DeviceIdType.MESH
NT = (((1,), (1,)), ((), ()))
NN = (((1,), (0,)), ((), ()))


def dot(a, b, dims=NN, precision=None):
    return lax.dot_general(a, b, dims, precision=precision, preferred_element_type=F32)


def iota(shape, axis):
    return lax.broadcasted_iota(jnp.int32, shape, axis)


def gather_kernel(
    green_block_hbm, own_chol, green_one_hbm, screening_hbm, chol_p, dressed, collision,
    green_block, green_one, screening, chol_t, part, part_in, ysum, y_in, z_all, vec, vx, vy, vz, uvec, uc,
    in_sem, own_send, own_recv, pc_send, pc_recv, z_send, z_recv, r_send, ready, uc_send, uc_recv, u_send, u_recv,
    x_send, x_recv, y_send, y_recv, l_send, l_recv, gy_send, gy_recv, gx_send, gx_recv,
    vx_send, vx_recv, vy_send, vy_recv, vz_send, vz_recv,
):
    row, aux = lax.axis_index("rows"), lax.axis_index("aux")
    mx, my, mz = row // (NY * NZ), (row // NZ) % NY, row % NZ
    mh, core = aux // 2, aux % 2

    def at_x(j):
        return {"rows": (((mx + j) % NX) * NY + my) * NZ + mz, "aux": aux}

    def at_y(j):
        return {"rows": (mx * NY + (my + j) % NY) * NZ + mz, "aux": aux}

    def at_z(j):
        return {"rows": (mx * NY + my) * NZ + (mz + j) % NZ, "aux": aux}

    def at(h):
        return {"rows": row, "aux": h * 2 + core}

    mate = {"rows": row, "aux": mh * 2 + 1 - core}
    sent = []

    def copy(src, dst, send, recv, to):
        return pltpu.make_async_remote_copy(
            src_ref=src, dst_ref=dst, send_sem=send, recv_sem=recv, device_id=to, device_id_type=MESH
        )

    def send(*what, when=None):
        made = copy(*what)
        sent.append((made, when))
        if when is None:
            made.start()
        else:
            pl.when(when)(made.start)

    odd, upper_half = mh % 2, mh // 2
    even, second, last = mh % 2 == 0, mh == 1, mh == NH - 1
    passes = jnp.logical_and(even, core == upper_half)

    barrier = pltpu.get_barrier_semaphore()
    peers = [at_y(j) for j in (4, 3, 5, 2, 6, 1, 7)] + [at_z(j) for j in range(1, NZ)]
    peers += [at_x(j) for j in (2, 1, 3)] + [mate]

    @pl.when(mh < NH - 1)
    def _():
        for step in (1, 3):
            pl.semaphore_signal(barrier, inc=1, device_id=at((mh + step) % NH), device_id_type=MESH)

    for peer in peers:
        pl.semaphore_signal(barrier, inc=1, device_id=peer, device_id_type=MESH)
    loads = [
        pltpu.make_async_copy(own_chol, chol_t.at[0, core], in_sem.at[0]),
        pltpu.make_async_copy(green_one_hbm, green_one, in_sem.at[1]),
        pltpu.make_async_copy(screening_hbm, screening, in_sem.at[2]),
        pltpu.make_async_copy(green_block_hbm, green_block, in_sem.at[3]),
    ]
    for load in loads:
        load.start()
    for load in loads:
        load.wait()

    pick = (iota((8, 256), 1) == aux).astype(F32)
    column = dot(pick, green_one[...], NT, HIGHEST)
    trace_row = dot(column, green_one[...], NT, HIGHEST)

    def split(value):
        wide = jnp.broadcast_to(value, (16, value.shape[1]))
        high = wide.astype(BF16).astype(F32)
        mid = (wide - high).astype(BF16).astype(F32)
        rest = wide - high - mid
        at_row = iota(wide.shape, 0)
        picked = jnp.where(at_row == 0, high, jnp.where(at_row == 1, mid, jnp.where(at_row == 2, rest, 0.0)))
        return picked.astype(BF16)

    def exact(value, right, dims):
        return jnp.sum(dot(split(value), right, dims), axis=0, keepdims=True)

    homes = (mh, 1 - odd, 2 - 2 * upper_half * (1 - odd), 3 - 2 * upper_half * odd)
    sub, lane = iota((8, 128), 0), iota((8, 128), 1)
    top = sub < 4

    own_first = 4 * (mx * NY + my)
    weights = [screening[pl.ds(home, 1), :] for home in homes]
    scales = [
        jnp.sum(jnp.where(lane == own_first + sub % 4, jnp.broadcast_to(w, (8, 128)), 0.0), axis=1, keepdims=True)
        for w in weights
    ]

    traced_rows = exact(trace_row[0:1, :], green_block[...], NT)
    tile = jnp.zeros((8, 128), F32)
    for r in range(4):
        tile = jnp.where(sub == r, jnp.broadcast_to(traced_rows[:, 128 * r : 128 * r + 128], (8, 128)), tile)
    uc[0] = tile

    pl.semaphore_wait(barrier, len(peers) + 1 + odd)

    @pl.when(last)
    def _():
        for h in (0, 2):
            pl.semaphore_signal(ready, inc=1, device_id=at(h), device_id_type=MESH)

    size = 64 // CHUNKS

    def block(t, i):
        return chol_t.at[t, core, pl.ds(i * size, size)]

    first_to, first_slot = 1 - odd, (1 - odd) * (1 + upper_half) + odd * mh
    for i in range(CHUNKS):
        send(block(0, i), block(first_slot, i), z_send.at[0, i], z_recv.at[first_slot, i], at(first_to))
        send(block(0, i), block(mh, i), z_send.at[1, i], z_recv.at[mh, i], at(2), when=odd == 1)
    send(chol_t.at[0, core], chol_t.at[0, core], own_send, own_recv, mate)
    send(uc.at[0], uc.at[1], uc_send, uc_recv, mate)

    def arrive(t, to=None, slot=None, when=None, u_when=None):
        for i in range(CHUNKS):
            here = block(t, i)
            copy(here, here, r_send.at[t, i], z_recv.at[t, i], mate).wait_recv()
            send(here, here, pc_send.at[t, i], pc_recv.at[t, i], mate)
            send(here, block(slot, i), r_send.at[t, i], z_recv.at[slot, i], at(to), when=when)
        copy(uvec.at[t], uvec.at[t], u_send.at[t], u_recv.at[t], mate).wait_recv()
        send(uvec.at[t], uvec.at[slot], u_send.at[t], u_recv.at[slot], at(to), when=u_when)

    def from_mate(t):
        for i in range(CHUNKS):
            there = chol_t.at[t, 1 - core, pl.ds(i * size, size)]
            copy(there, there, pc_send.at[t, i], pc_recv.at[t, i], mate).wait_recv()

    def project(t):
        product = dot(chol_t[t].reshape(128, 512), green_block[...])
        for j in range(16):
            left, right = product[8 * j : 8 * j + 8, :128], product[8 * j : 8 * j + 8, 128:]
            for e in range(2):
                g = 2 * j + e
                if e == 0:
                    tile = jnp.where(top, left, pltpu.roll(right, 4, 0))
                else:
                    tile = jnp.where(top, pltpu.roll(left, 4, 0), right)
                part[t, g // NY, g % NY] = tile
        for j in (2, 1, 3):
            send(part.at[t, (mx + j) % NX], part_in.at[t, j], x_send.at[t, j], x_recv.at[t, j], at_x(j))

    def sum_x(t):
        total = part[t, mx]
        for j in range(1, NX):
            copy(part_in.at[t, j], part_in.at[t, j], x_send.at[t, j], x_recv.at[t, j], mate).wait_recv()
            total = total + part_in[t, j]
        ysum[t] = total
        for j in (4, 3, 5, 2, 6, 1, 7):
            send(ysum.at[t, (my + j) % NY], y_in.at[t, j], y_send.at[t, j], y_recv.at[t, j], at_y(j))

    def sum_y(t):
        total = ysum[t, my]
        for j in range(1, NY):
            copy(y_in.at[t, j], y_in.at[t, j], y_send.at[t, j], y_recv.at[t, j], mate).wait_recv()
            total = total + y_in[t, j]
        z_all[mz, t] = total
        for j in range(1, NZ):
            send(z_all.at[mz, t], z_all.at[mz, t], l_send.at[t, j], l_recv.at[t, j], at_z(j))

    def spread(value, store, sems, count, to):
        store[0] = value
        for j in range(1, count):
            send(store.at[0], store.at[j], sems[0].at[j], sems[1].at[j], to(j))

    def collect(store, sems, count):
        total = store[0]
        for j in range(1, count):
            copy(store.at[j], store.at[j], sems[0].at[j], sems[1].at[j], mate).wait_recv()
            total = total + store[j]
        return total

    there = chol_t.at[0, 1 - core]
    copy(there, there, own_send, own_recv, mate).wait_recv()
    project(0)
    copy(uc.at[1], uc.at[1], uc_send, uc_recv, mate).wait_recv()
    uvec[0] = uc[0] + uc[1]
    send(uvec.at[0], uvec.at[first_slot], u_send.at[4], u_recv.at[first_slot], at(first_to))
    send(uvec.at[0], uvec.at[mh], u_send.at[5], u_recv.at[mh], at(2), when=odd == 1)

    arrive(1, 2, 2, second, second)
    from_mate(1)
    project(1)
    arrive(2, 0, 2, second, second)
    from_mate(2)
    project(2)

    @pl.when(even)
    def _():
        pl.semaphore_wait(ready, 1)

    late_slot = 1 + upper_half
    for i in range(CHUNKS):
        send(block(0, i), block(late_slot, i), z_send.at[2, i], z_recv.at[late_slot, i], at(3), when=even)
        send(block(1, i), block(3, i), z_send.at[3, i], z_recv.at[3, i], at(3), when=passes)
    send(uvec.at[0], uvec.at[late_slot], u_send.at[6], u_recv.at[late_slot], at(3), when=even)
    send(uvec.at[1], uvec.at[3], u_send.at[7], u_recv.at[3], at(3), when=mh == 0)
    sum_x(0)
    sum_x(1)
    sum_y(0)
    arrive(3, 1, 3, passes, mh == 0)
    from_mate(3)
    project(3)

    all_rows = (uvec[0] + uvec[1]) + (uvec[2] + uvec[3])
    all_row = jnp.concatenate([all_rows[r : r + 1, :] for r in range(4)], axis=1)
    tile = jnp.zeros((8, 128), F32)
    for t in range(4):
        tile = jnp.where(sub == t, jnp.broadcast_to(exact(all_row, chol_t[t].reshape(128, 512), NT), (8, 128)), tile)
    sems_vx, sems_vy, sems_vz = (vx_send, vx_recv), (vy_send, vy_recv), (vz_send, vz_recv)
    spread(tile, vx, sems_vx, NX, at_x)
    sum_x(2)
    sum_x(3)
    spread(collect(vx, sems_vx, NX), vy, sems_vy, NY, at_y)

    for b in range(4):
        new = iota((128, 512), 0) + 128 * b
        old = ((new >> 2) & 3) * 128 + (new >> 7) * 32 + ((new >> 4) & 7) * 4 + (new & 3)
        move = jnp.where(iota((128, 512), 1) == old, 1.0, 0.0).astype(BF16)
        moved = dot(move, chol_t[...].reshape(512, 512))
        chol_p[:, 128 * b : 128 * b + 128] = moved.T.astype(BF16)

    sum_y(1)
    sum_y(2)
    sum_y(3)
    spread(collect(vy, sems_vy, NY), vz, sems_vz, NZ, at_z)

    for t in range(4):
        for j in range(1, NZ):
            there = z_all.at[(mz + NZ - j) % NZ, t]
            copy(there, there, l_send.at[t, j], l_recv.at[t, j], mate).wait_recv()
    total = (z_all[0] + z_all[1]) + (z_all[2] + z_all[3])
    flat = total.reshape(32, 128)
    upper = dot(flat, green_one[:128, :], NN, HIGHEST)
    lower = dot(flat, green_one[128:, :], NN, HIGHEST)
    done = []
    for t in range(4):
        both = upper[8 * t : 8 * t + 8] + pltpu.roll(lower[8 * t : 8 * t + 8], 4, 0)
        done.append(both * scales[t])
    top2 = iota((8, 256), 0) < 4
    first = jnp.where(top2, done[0], pltpu.roll(done[1], 4, 0))
    second = jnp.where(top2, done[2], pltpu.roll(done[3], 4, 0))
    dressed[mx, my] = jnp.concatenate([first, second], axis=0).astype(BF16)

    def along_x(j):
        here = dressed.at[mx, (my + NY - j) % NY]
        for i in (2, 1, 3):
            send(here, here, gx_send.at[j, i], gx_recv.at[j, i], at_x(i))

    order = (1, 7, 2, 6, 3, 5, 4)
    here = dressed.at[mx, my]
    for j in order[::-1]:
        send(here, here, gy_send.at[j], gy_recv.at[j], at_y(j))
    along_x(0)
    vec[...] = collect(vz, sems_vz, NZ)
    traced = jnp.zeros((1, 512), F32)
    for t in range(4):
        traced = traced + exact(vec[t : t + 1, :] * weights[t], chol_t[t].reshape(128, 512), NN)
    for a in range(2 * NH):
        @pl.when(aux == a)
        def _():
            collision[...] = traced[:, 64 * a : 64 * a + 64]

    for j in order:
        there = dressed.at[mx, (my + NY - j) % NY]
        copy(there, there, gy_send.at[j], gy_recv.at[j], mate).wait_recv()
        along_x(j)

    for i in range(1, NX):
        for j in range(NY):
            there = dressed.at[(mx + NX - i) % NX, (my + NY - j) % NY]
            copy(there, there, gx_send.at[j, i], gx_recv.at[j, i], mate).wait_recv()

    for made, when in sent:
        if when is None:
            made.wait_send()
        else:
            pl.when(when)(made.wait_send)


SEMS = (
    (4,), (), (), (4, CHUNKS), (4, CHUNKS), (4, CHUNKS), (4, CHUNKS), (4, CHUNKS), None, (), (), (8,), (4,),
    (4, NX), (4, NX), (4, NY), (4, NY), (4, NZ), (4, NZ), (NY,), (NY,), (NY, NX), (NY, NX),
    (NX,), (NX,), (NY,), (NY,), (NZ,), (NZ,),
)


def local(pair_green_block, cholesky_factors, green_one, screening):
    vmem, dma = pltpu.VMEM, pltpu.SemaphoreType.DMA
    tile = (8, 128)
    chol_p, dressed, collision = pl.pallas_call(
        gather_kernel,
        out_shape=(
            pltpu.VMEM((512, 512), BF16),
            pltpu.VMEM((NX, NY, 16, 256), BF16),
            pltpu.VMEM((1, 64), F32),
        ),
        in_specs=[pl.BlockSpec(memory_space=pl.ANY)] * 4,
        out_specs=(pl.BlockSpec(memory_space=vmem),) * 3,
        scratch_shapes=[
            vmem((512, 256), BF16), vmem((256, 256), F32), vmem((4, 128), F32),
            vmem((4, 2, 64, 512), BF16),
            vmem((4, NX, NY) + tile, F32),
            vmem((4, NX, NY) + tile, F32),
            vmem((4, NY) + tile, F32),
            vmem((4, NY) + tile, F32),
            vmem((NZ, 4) + tile, F32),
            vmem(tile, F32),
            vmem((NX,) + tile, F32), vmem((NY,) + tile, F32), vmem((NZ,) + tile, F32), vmem((4,) + tile, F32), vmem((2,) + tile, F32),
        ] + [pltpu.SemaphoreType.REGULAR if shape is None else dma(shape) for shape in SEMS],
        compiler_params=pltpu.CompilerParams(collective_id=0, has_side_effects=True),
    )(pair_green_block, cholesky_factors.T, green_one, screening.reshape(4, 128))
    slope = jnp.dot(chol_p, dressed.reshape(512, 256), preferred_element_type=F32)
    return slope, collision.reshape(64)


def solution(mesh):
    placed = (P("rows", "aux"), P("rows", "aux"), P(), P())
    return jax.shard_map(
        local,
        mesh=mesh,
        in_specs=placed,
        out_specs=(P("rows", "aux"), P(("rows", "aux"))),
        check_vma=False,
    )
```

```python
import jax
import jax.numpy as jnp
from jax import lax
from jax.experimental import pallas as pl
from jax.experimental.pallas import tpu as pltpu
from jax.sharding import PartitionSpec as P

NX, NY, NZ, NH = 4, 8, 4, 4
CHUNKS = 2
F32, BF16 = jnp.float32, jnp.bfloat16
HIGHEST = lax.Precision.HIGHEST
MESH = pl.DeviceIdType.MESH
NT = (((1,), (1,)), ((), ()))
NN = (((1,), (0,)), ((), ()))


def dot(a, b, dims=NN, precision=None):
    return lax.dot_general(a, b, dims, precision=precision, preferred_element_type=F32)


def iota(shape, axis):
    return lax.broadcasted_iota(jnp.int32, shape, axis)


def gather_kernel(
    green_block_hbm, own_chol, green_one_hbm, screening_hbm, chol_p, dressed, collision,
    green_block, green_one, screening, chol_t, part, part_in, ysum, y_in, z_all, vec, vx, vy, vz, uvec, uc,
    in_sem, own_send, own_recv, pc_send, pc_recv, z_send, z_recv, f_send, uc_send, uc_recv, u_send, u_recv,
    x_send, x_recv, y_send, y_recv, l_send, l_recv, gy_send, gy_recv, gx_send, gx_recv,
    vx_send, vx_recv, vy_send, vy_recv, vz_send, vz_recv,
):
    row, aux = lax.axis_index("rows"), lax.axis_index("aux")
    mx, my, mz = row // (NY * NZ), (row // NZ) % NY, row % NZ
    mh, core = aux // 2, aux % 2

    def at_x(j):
        return {"rows": (((mx + j) % NX) * NY + my) * NZ + mz, "aux": aux}

    def at_y(j):
        return {"rows": (mx * NY + (my + j) % NY) * NZ + mz, "aux": aux}

    def at_z(j):
        return {"rows": (mx * NY + my) * NZ + (mz + j) % NZ, "aux": aux}

    def at_h(j):
        return {"rows": row, "aux": ((mh + j) % NH) * 2 + core}

    mate = {"rows": row, "aux": mh * 2 + 1 - core}
    sent = []

    def copy(src, dst, send, recv, to):
        return pltpu.make_async_remote_copy(
            src_ref=src, dst_ref=dst, send_sem=send, recv_sem=recv, device_id=to, device_id_type=MESH
        )

    def send(*what):
        made = copy(*what)
        made.start()
        sent.append(made)
        return made

    barrier = pltpu.get_barrier_semaphore()
    peers = [at_h(1), at_h(NH - 1)] + [at_y(j) for j in (4, 3, 5, 2, 6, 1, 7)]
    peers += [at_z(j) for j in range(1, NZ)] + [at_x(j) for j in (2, 1, 3)] + [mate]
    for peer in peers:
        pl.semaphore_signal(barrier, inc=1, device_id=peer, device_id_type=MESH)
    loads = [
        pltpu.make_async_copy(own_chol, chol_t.at[0, core], in_sem.at[0]),
        pltpu.make_async_copy(green_one_hbm, green_one, in_sem.at[1]),
        pltpu.make_async_copy(screening_hbm, screening, in_sem.at[2]),
        pltpu.make_async_copy(green_block_hbm, green_block, in_sem.at[3]),
    ]
    for load in loads:
        load.start()
    pl.semaphore_wait(barrier, len(peers))

    size = 64 // CHUNKS
    onward, back = at_h(1 + 2 * core), at_h(3 - 2 * core)
    for i in range(CHUNKS):
        span = pl.ds(i * size, size)
        mine = own_chol.at[span]
        send(mine, chol_t.at[1, core, span], z_send.at[0, i], z_recv.at[1, i], onward)
        send(mine, chol_t.at[2, core, span], z_send.at[1, i], z_recv.at[2, i], back)
    send(own_chol, chol_t.at[0, core], own_send, own_recv, mate)

    for load in loads:
        load.wait()

    pick = (iota((8, 256), 1) == aux).astype(F32)
    column = dot(pick, green_one[...], NT, HIGHEST)
    trace_row = dot(column, green_one[...], NT, HIGHEST)

    def split(value):
        wide = jnp.broadcast_to(value, (16, value.shape[1]))
        high = wide.astype(BF16).astype(F32)
        mid = (wide - high).astype(BF16).astype(F32)
        rest = wide - high - mid
        at_row = iota(wide.shape, 0)
        picked = jnp.where(at_row == 0, high, jnp.where(at_row == 1, mid, jnp.where(at_row == 2, rest, 0.0)))
        return picked.astype(BF16)

    def exact(value, right, dims):
        return jnp.sum(dot(split(value), right, dims), axis=0, keepdims=True)

    before, after, across = (mh + NH - 1) % NH, (mh + 1) % NH, (mh + 2) % NH
    homes = ((mh, mh), (before, after), (after, before), (across, across))
    sub, lane = iota((8, 128), 0), iota((8, 128), 1)
    top, low = sub < 4, lane < 64

    def by_piece(t, read):
        first = jnp.broadcast_to(read(homes[t][0]), (8, 128))
        second = jnp.broadcast_to(read(homes[t][1]), (8, 128))
        return jnp.where(low, first, second)

    own_first = 4 * (mx * NY + my)
    weights = [by_piece(t, lambda h: screening[pl.ds(h, 1), :]) for t in range(4)]
    scales = [jnp.sum(jnp.where(lane == own_first + sub % 4, w, 0.0), axis=1, keepdims=True) for w in weights]

    traced_rows = exact(trace_row[0:1, :], green_block[...], NT)
    tile = jnp.zeros((8, 128), F32)
    for r in range(4):
        tile = jnp.where(sub == r, jnp.broadcast_to(traced_rows[:, 128 * r : 128 * r + 128], (8, 128)), tile)
    uc[0] = tile
    send(uc.at[0], uc.at[1], uc_send, uc_recv, mate)

    def await_z(t, i):
        here = chol_t.at[t, core, pl.ds(i * size, size)]
        copy(here, here, f_send.at[i], z_recv.at[t, i], mate).wait_recv()
        return here

    def to_mate(t, i, here):
        send(here, here, pc_send.at[t, i], pc_recv.at[t, i], mate)

    def from_mate(t):
        for i in range(CHUNKS):
            there = chol_t.at[t, 1 - core, pl.ds(i * size, size)]
            copy(there, there, pc_send.at[t, i], pc_recv.at[t, i], mate).wait_recv()

    def project(t):
        block = dot(chol_t[t].reshape(128, 512), green_block[...])
        for j in range(16):
            left, right = block[8 * j : 8 * j + 8, :128], block[8 * j : 8 * j + 8, 128:]
            for e in range(2):
                g = 2 * j + e
                if e == 0:
                    tile = jnp.where(top, left, pltpu.roll(right, 4, 0))
                else:
                    tile = jnp.where(top, pltpu.roll(left, 4, 0), right)
                part[t, g // NY, g % NY] = tile
        for j in (2, 1, 3):
            send(part.at[t, (mx + j) % NX], part_in.at[t, j], x_send.at[t, j], x_recv.at[t, j], at_x(j))

    def sum_x(t):
        total = part[t, mx]
        for j in range(1, NX):
            copy(part_in.at[t, j], part_in.at[t, j], x_send.at[t, j], x_recv.at[t, j], mate).wait_recv()
            total = total + part_in[t, j]
        ysum[t] = total
        for j in (4, 3, 5, 2, 6, 1, 7):
            send(ysum.at[t, (my + j) % NY], y_in.at[t, j], y_send.at[t, j], y_recv.at[t, j], at_y(j))

    def sum_y(t):
        total = ysum[t, my]
        for j in range(1, NY):
            copy(y_in.at[t, j], y_in.at[t, j], y_send.at[t, j], y_recv.at[t, j], mate).wait_recv()
            total = total + y_in[t, j]
        z_all[mz, t] = total
        for j in range(1, NZ):
            send(z_all.at[mz, t], z_all.at[mz, t], l_send.at[t, j], l_recv.at[t, j], at_z(j))

    def spread(value, store, sems, count, to):
        store[0] = value
        for j in range(1, count):
            send(store.at[0], store.at[j], sems[0].at[j], sems[1].at[j], to(j))

    def collect(store, sems, count):
        total = store[0]
        for j in range(1, count):
            copy(store.at[j], store.at[j], sems[0].at[j], sems[1].at[j], mate).wait_recv()
            total = total + store[j]
        return total

    def await_u(t):
        copy(uvec.at[t], uvec.at[t], u_send.at[0], u_recv.at[t], mate).wait_recv()

    there = chol_t.at[0, 1 - core]
    copy(there, there, own_send, own_recv, mate).wait_recv()
    project(0)
    copy(uc.at[1], uc.at[1], uc_send, uc_recv, mate).wait_recv()
    uvec[0] = uc[0] + uc[1]
    send(uvec.at[0], uvec.at[1], u_send.at[0], u_recv.at[1], at_h(1))
    send(uvec.at[0], uvec.at[2], u_send.at[1], u_recv.at[2], at_h(3))

    for i in range(CHUNKS):
        here = await_z(1, i)
        send(here, chol_t.at[3, core, pl.ds(i * size, size)], f_send.at[i], z_recv.at[3, i], onward)
        to_mate(1, i, here)
    await_u(1)
    send(uvec.at[1], uvec.at[3], u_send.at[2], u_recv.at[3], at_h(1))
    for i in range(CHUNKS):
        to_mate(2, i, await_z(2, i))
    await_u(2)
    from_mate(1)
    project(1)
    from_mate(2)
    project(2)
    sum_x(0)
    for i in range(CHUNKS):
        to_mate(3, i, await_z(3, i))
    await_u(3)
    from_mate(3)
    project(3)

    all_rows = (uvec[0] + uvec[1]) + (uvec[2] + uvec[3])
    all_row = jnp.concatenate([all_rows[r : r + 1, :] for r in range(4)], axis=1)
    tile = jnp.zeros((8, 128), F32)
    for t in range(4):
        tile = jnp.where(sub == t, jnp.broadcast_to(exact(all_row, chol_t[t].reshape(128, 512), NT), (8, 128)), tile)
    sems_vx, sems_vy, sems_vz = (vx_send, vx_recv), (vy_send, vy_recv), (vz_send, vz_recv)
    spread(tile, vx, sems_vx, NX, at_x)
    sum_x(1)
    sum_x(2)
    sum_x(3)
    sum_y(0)
    spread(collect(vx, sems_vx, NX), vy, sems_vy, NY, at_y)

    for b in range(4):
        new = iota((128, 512), 0) + 128 * b
        old = ((new >> 2) & 3) * 128 + (new >> 7) * 32 + ((new >> 4) & 7) * 4 + (new & 3)
        move = jnp.where(iota((128, 512), 1) == old, 1.0, 0.0).astype(BF16)
        moved = dot(move, chol_t[...].reshape(512, 512))
        chol_p[:, 128 * b : 128 * b + 128] = moved.T.astype(BF16)

    sum_y(1)
    sum_y(2)
    sum_y(3)
    spread(collect(vy, sems_vy, NY), vz, sems_vz, NZ, at_z)

    for t in range(4):
        for j in range(1, NZ):
            there = z_all.at[(mz + NZ - j) % NZ, t]
            copy(there, there, l_send.at[t, j], l_recv.at[t, j], mate).wait_recv()
    total = (z_all[0] + z_all[1]) + (z_all[2] + z_all[3])
    flat = total.reshape(32, 128)
    upper = dot(flat, green_one[:128, :], NN, HIGHEST)
    lower = dot(flat, green_one[128:, :], NN, HIGHEST)
    done = []
    for t in range(4):
        both = upper[8 * t : 8 * t + 8] + pltpu.roll(lower[8 * t : 8 * t + 8], 4, 0)
        done.append(both * scales[t])
    top2 = iota((8, 256), 0) < 4
    first = jnp.where(top2, done[0], pltpu.roll(done[1], 4, 0))
    second = jnp.where(top2, done[2], pltpu.roll(done[3], 4, 0))
    dressed[mx, my] = jnp.concatenate([first, second], axis=0).astype(BF16)

    def along_x(j):
        here = dressed.at[mx, (my + NY - j) % NY]
        for i in (2, 1, 3):
            send(here, here, gx_send.at[j, i], gx_recv.at[j, i], at_x(i))

    order = (1, 7, 2, 6, 3, 5, 4)
    here = dressed.at[mx, my]
    for j in order[::-1]:
        send(here, here, gy_send.at[j], gy_recv.at[j], at_y(j))
    along_x(0)
    vec[...] = collect(vz, sems_vz, NZ)
    for j in order:
        there = dressed.at[mx, (my + NY - j) % NY]
        copy(there, there, gy_send.at[j], gy_recv.at[j], mate).wait_recv()
        along_x(j)

    traced = jnp.zeros((1, 512), F32)
    for t in range(4):
        traced = traced + exact(vec[t : t + 1, :] * weights[t][0:1, :], chol_t[t].reshape(128, 512), NN)
    for a in range(2 * NH):
        @pl.when(aux == a)
        def _():
            collision[...] = traced[:, 64 * a : 64 * a + 64]

    for i in range(1, NX):
        for j in range(NY):
            there = dressed.at[(mx + NX - i) % NX, (my + NY - j) % NY]
            copy(there, there, gx_send.at[j, i], gx_recv.at[j, i], mate).wait_recv()

    for made in sent:
        made.wait_send()


SEMS = (
    (4,), (), (), (4, CHUNKS), (4, CHUNKS), (2, CHUNKS), (4, CHUNKS), (CHUNKS,), (), (), (3,), (4,),
    (4, NX), (4, NX), (4, NY), (4, NY), (4, NZ), (4, NZ), (NY,), (NY,), (NY, NX), (NY, NX),
    (NX,), (NX,), (NY,), (NY,), (NZ,), (NZ,),
)


def local(pair_green_block, cholesky_factors, green_one, screening):
    vmem, dma = pltpu.VMEM, pltpu.SemaphoreType.DMA
    tile = (8, 128)
    chol_p, dressed, collision = pl.pallas_call(
        gather_kernel,
        out_shape=(
            pltpu.VMEM((512, 512), BF16),
            pltpu.VMEM((NX, NY, 16, 256), BF16),
            pltpu.VMEM((1, 64), F32),
        ),
        in_specs=[pl.BlockSpec(memory_space=pl.ANY)] * 4,
        out_specs=(pl.BlockSpec(memory_space=vmem),) * 3,
        scratch_shapes=[
            vmem((512, 256), BF16), vmem((256, 256), F32), vmem((4, 128), F32),
            vmem((4, 2, 64, 512), BF16),
            vmem((4, NX, NY) + tile, F32),
            vmem((4, NX, NY) + tile, F32),
            vmem((4, NY) + tile, F32),
            vmem((4, NY) + tile, F32),
            vmem((NZ, 4) + tile, F32),
            vmem(tile, F32),
            vmem((NX,) + tile, F32), vmem((NY,) + tile, F32), vmem((NZ,) + tile, F32), vmem((4,) + tile, F32),
            vmem((2,) + tile, F32),
        ] + [dma(shape) for shape in SEMS],
        compiler_params=pltpu.CompilerParams(collective_id=0, has_side_effects=True),
    )(pair_green_block, cholesky_factors.T, green_one, screening.reshape(4, 128))
    slope = jnp.dot(chol_p, dressed.reshape(512, 256), preferred_element_type=F32)
    return slope, collision.reshape(64)


def solution(mesh):
    placed = (P("rows", "aux"), P("rows", "aux"), P(), P())
    return jax.shard_map(
        local,
        mesh=mesh,
        in_specs=placed,
        out_specs=(P("rows", "aux"), P(("rows", "aux"))),
        check_vma=False,
    )
```

```python
import jax
import jax.numpy as jnp
from jax import lax
from jax.experimental import pallas as pl
from jax.experimental.pallas import tpu as pltpu
from jax.sharding import PartitionSpec as P

NX, NY, NZ, NH = 4, 8, 4, 4
CHUNKS = 2
F32, BF16 = jnp.float32, jnp.bfloat16
HIGHEST = lax.Precision.HIGHEST
MESH = pl.DeviceIdType.MESH
NT = (((1,), (1,)), ((), ()))
NN = (((1,), (0,)), ((), ()))


def dot(a, b, dims=NN, precision=None):
    return lax.dot_general(a, b, dims, precision=precision, preferred_element_type=F32)


def iota(shape, axis):
    return lax.broadcasted_iota(jnp.int32, shape, axis)


def gather_kernel(
    green_block_hbm, own_chol, green_one_hbm, screening_hbm, chol_p, dressed, collision,
    green_block, green_one, screening, chol_t, part, part_in, ysum, y_in, z_all, vec, vx, vy, vz, uvec, uc,
    in_sem, own_send, own_recv, pc_send, pc_recv, z_send, z_recv, r_send, ready, uc_send, uc_recv, u_send, u_recv,
    tok_x, tok_y, tok_z,
    x_send, x_recv, y_send, y_recv, l_send, l_recv, gy_send, gy_recv, gx_send, gx_recv,
    vx_send, vx_recv, vy_send, vy_recv, vz_send, vz_recv,
):
    row, aux = lax.axis_index("rows"), lax.axis_index("aux")
    mx, my, mz = row // (NY * NZ), (row // NZ) % NY, row % NZ
    mh, core = aux // 2, aux % 2

    def at_x(j):
        return {"rows": (((mx + j) % NX) * NY + my) * NZ + mz, "aux": aux}

    def at_y(j):
        return {"rows": (mx * NY + (my + j) % NY) * NZ + mz, "aux": aux}

    def at_z(j):
        return {"rows": (mx * NY + my) * NZ + (mz + j) % NZ, "aux": aux}

    def at(h):
        return {"rows": row, "aux": h * 2 + core}

    mate = {"rows": row, "aux": mh * 2 + 1 - core}
    sent = []

    def copy(src, dst, send, recv, to):
        return pltpu.make_async_remote_copy(
            src_ref=src, dst_ref=dst, send_sem=send, recv_sem=recv, device_id=to, device_id_type=MESH
        )

    def send(*what, when=None):
        made = copy(*what)
        sent.append((made, when))
        if when is None:
            made.start()
        else:
            pl.when(when)(made.start)

    odd, upper_half = mh % 2, mh // 2
    even, second, last = mh % 2 == 0, mh == 1, mh == NH - 1
    passes = jnp.logical_and(even, core == upper_half)

    barrier = pltpu.get_barrier_semaphore()
    peers = [at_y(1), at_y(NY - 1), at_x(1), at_x(NX - 1), mate]
    has_down, has_up = mz > 0, mz < NZ - 1
    line = ((has_down, at_z(NZ - 1), 0), (has_up, at_z(1), 1))

    def signal(sem, to):
        pl.semaphore_signal(sem, inc=1, device_id=to, device_id_type=MESH)

    @pl.when(mh < NH - 1)
    def _():
        for step in (1, 3):
            signal(barrier, at((mh + step) % NH))

    for there, to, _ in line:
        pl.when(there)(lambda to=to: signal(barrier, to))
    for peer in peers:
        signal(barrier, peer)
    loads = [
        pltpu.make_async_copy(own_chol, chol_t.at[0, core], in_sem.at[0]),
        pltpu.make_async_copy(green_one_hbm, green_one, in_sem.at[1]),
        pltpu.make_async_copy(screening_hbm, screening, in_sem.at[2]),
        pltpu.make_async_copy(green_block_hbm, green_block, in_sem.at[3]),
    ]
    for load in loads:
        load.start()
    inner = has_down.astype(jnp.int32) + has_up.astype(jnp.int32)
    pl.semaphore_wait(barrier, len(peers) + 1 + odd + inner)

    @pl.when(last)
    def _():
        for h in (0, 2):
            signal(ready, at(h))

    size = 64 // CHUNKS

    def block(t, i):
        return chol_t.at[t, core, pl.ds(i * size, size)]

    first_to, first_slot = 1 - odd, (1 - odd) * (1 + upper_half) + odd * mh
    for i in range(CHUNKS):
        mine = own_chol.at[pl.ds(i * size, size)]
        send(mine, block(first_slot, i), z_send.at[0, i], z_recv.at[first_slot, i], at(first_to))
    for i in range(CHUNKS):
        mine = own_chol.at[pl.ds(i * size, size)]
        send(mine, block(mh, i), z_send.at[1, i], z_recv.at[mh, i], at(2), when=odd == 1)
    send(own_chol, chol_t.at[0, core], own_send, own_recv, mate)

    def announce(y=True, z=True):
        if y:
            signal(tok_y.at[0], at_y(1))
            signal(tok_y.at[1], at_y(NY - 1))
        if z:
            for there, to, side in line:
                pl.when(there)(lambda to=to, side=side: signal(tok_z.at[side], to))

    def heard(y=True, z=True):
        if y:
            pl.semaphore_wait(tok_y.at[0], 1)
            pl.semaphore_wait(tok_y.at[1], 1)
        if z:
            for there, _, side in line:
                pl.when(there)(lambda side=side: pl.semaphore_wait(tok_z.at[1 - side], 1))

    signal(tok_x, at_x(1))
    announce()
    for load in loads:
        load.wait()

    pick = (iota((8, 256), 1) == aux).astype(F32)
    column = dot(pick, green_one[...], NT, HIGHEST)
    trace_row = dot(column, green_one[...], NT, HIGHEST)

    def split(value):
        wide = jnp.broadcast_to(value, (16, value.shape[1]))
        high = wide.astype(BF16).astype(F32)
        mid = (wide - high).astype(BF16).astype(F32)
        rest = wide - high - mid
        at_row = iota(wide.shape, 0)
        picked = jnp.where(at_row == 0, high, jnp.where(at_row == 1, mid, jnp.where(at_row == 2, rest, 0.0)))
        return picked.astype(BF16)

    def exact(value, right, dims):
        return jnp.sum(dot(split(value), right, dims), axis=0, keepdims=True)

    homes = (mh, 1 - odd, 2 - 2 * upper_half * (1 - odd), 3 - 2 * upper_half * odd)
    sub, lane = iota((8, 128), 0), iota((8, 128), 1)
    top = sub < 4

    own_first = 4 * (mx * NY + my)
    weights = [screening[pl.ds(home, 1), :] for home in homes]
    scales = [
        jnp.sum(jnp.where(lane == own_first + sub % 4, jnp.broadcast_to(w, (8, 128)), 0.0), axis=1, keepdims=True)
        for w in weights
    ]

    traced_rows = exact(trace_row[0:1, :], green_block[...], NT)
    tile = jnp.zeros((8, 128), F32)
    for r in range(4):
        tile = jnp.where(sub == r, jnp.broadcast_to(traced_rows[:, 128 * r : 128 * r + 128], (8, 128)), tile)
    uc[0] = tile

    send(uc.at[0], uc.at[1], uc_send, uc_recv, mate)
    heard()
    announce()
    pl.semaphore_wait(tok_x, 1)

    def arrive(t, to=None, slot=None, when=None, u_when=None):
        for i in range(CHUNKS):
            here = block(t, i)
            copy(here, here, r_send.at[t, i], z_recv.at[t, i], mate).wait_recv()
            send(here, here, pc_send.at[t, i], pc_recv.at[t, i], mate)
            send(here, block(slot, i), r_send.at[t, i], z_recv.at[slot, i], at(to), when=when)
        copy(uvec.at[t], uvec.at[t], u_send.at[t], u_recv.at[t], mate).wait_recv()
        send(uvec.at[t], uvec.at[slot], u_send.at[t], u_recv.at[slot], at(to), when=u_when)

    def from_mate(t):
        for i in range(CHUNKS):
            there = chol_t.at[t, 1 - core, pl.ds(i * size, size)]
            copy(there, there, pc_send.at[t, i], pc_recv.at[t, i], mate).wait_recv()

    def project(t):
        product = dot(chol_t[t].reshape(128, 512), green_block[...])
        for j in range(16):
            left, right = product[8 * j : 8 * j + 8, :128], product[8 * j : 8 * j + 8, 128:]
            for e in range(2):
                g = 2 * j + e
                if e == 0:
                    tile = jnp.where(top, left, pltpu.roll(right, 4, 0))
                else:
                    tile = jnp.where(top, pltpu.roll(left, 4, 0), right)
                part[t, g // NY, g % NY] = tile
        for j in (2, 1, 3):
            send(part.at[t, (mx + j) % NX], part_in.at[t, j], x_send.at[t, j], x_recv.at[t, j], at_x(j))

    def sum_x(t):
        total = part[t, mx]
        for j in range(1, NX):
            copy(part_in.at[t, j], part_in.at[t, j], x_send.at[t, j], x_recv.at[t, j], mate).wait_recv()
            total = total + part_in[t, j]
        ysum[t] = total
        for j in (4, 3, 5, 2, 6, 1, 7):
            send(ysum.at[t, (my + j) % NY], y_in.at[t, j], y_send.at[t, j], y_recv.at[t, j], at_y(j))

    def sum_y(t):
        total = ysum[t, my]
        for j in range(1, NY):
            copy(y_in.at[t, j], y_in.at[t, j], y_send.at[t, j], y_recv.at[t, j], mate).wait_recv()
            total = total + y_in[t, j]
        z_all[mz, t] = total
        for j in range(1, NZ):
            send(z_all.at[mz, t], z_all.at[mz, t], l_send.at[t, j], l_recv.at[t, j], at_z(j))

    def spread(value, store, sems, count, to):
        store[0] = value
        for j in range(1, count):
            send(store.at[0], store.at[j], sems[0].at[j], sems[1].at[j], to(j))

    def collect(store, sems, count):
        total = store[0]
        for j in range(1, count):
            copy(store.at[j], store.at[j], sems[0].at[j], sems[1].at[j], mate).wait_recv()
            total = total + store[j]
        return total

    there = chol_t.at[0, 1 - core]
    copy(there, there, own_send, own_recv, mate).wait_recv()
    project(0)
    copy(uc.at[1], uc.at[1], uc_send, uc_recv, mate).wait_recv()
    uvec[0] = uc[0] + uc[1]
    send(uvec.at[0], uvec.at[first_slot], u_send.at[4], u_recv.at[first_slot], at(first_to))
    send(uvec.at[0], uvec.at[mh], u_send.at[5], u_recv.at[mh], at(2), when=odd == 1)

    heard()
    announce(z=False)
    heard(z=False)
    arrive(1, 2, 2, second, second)
    from_mate(1)
    project(1)

    @pl.when(even)
    def _():
        pl.semaphore_wait(ready, 1)

    late_slot = 1 + upper_half
    for i in range(CHUNKS):
        send(block(0, i), block(late_slot, i), z_send.at[2, i], z_recv.at[late_slot, i], at(3), when=even)
        send(block(1, i), block(3, i), z_send.at[3, i], z_recv.at[3, i], at(3), when=passes)
    send(uvec.at[0], uvec.at[late_slot], u_send.at[6], u_recv.at[late_slot], at(3), when=even)
    send(uvec.at[1], uvec.at[3], u_send.at[7], u_recv.at[3], at(3), when=mh == 0)
    arrive(2, 0, 2, second, second)
    arrive(3, 1, 3, passes, mh == 0)
    from_mate(2)
    project(2)
    from_mate(3)
    project(3)
    sum_x(0)

    all_rows = (uvec[0] + uvec[1]) + (uvec[2] + uvec[3])
    all_row = jnp.concatenate([all_rows[r : r + 1, :] for r in range(4)], axis=1)
    tile = jnp.zeros((8, 128), F32)
    for t in range(4):
        tile = jnp.where(sub == t, jnp.broadcast_to(exact(all_row, chol_t[t].reshape(128, 512), NT), (8, 128)), tile)
    sems_vx, sems_vy, sems_vz = (vx_send, vx_recv), (vy_send, vy_recv), (vz_send, vz_recv)
    spread(tile, vx, sems_vx, NX, at_x)
    sum_x(1)
    sum_x(2)
    sum_x(3)
    sum_y(0)
    spread(collect(vx, sems_vx, NX), vy, sems_vy, NY, at_y)

    for b in range(4):
        new = iota((128, 512), 0) + 128 * b
        old = ((new >> 2) & 3) * 128 + (new >> 7) * 32 + ((new >> 4) & 7) * 4 + (new & 3)
        move = jnp.where(iota((128, 512), 1) == old, 1.0, 0.0).astype(BF16)
        moved = dot(move, chol_t[...].reshape(512, 512))
        chol_p[:, 128 * b : 128 * b + 128] = moved.T.astype(BF16)

    sum_y(1)
    sum_y(2)
    sum_y(3)
    spread(collect(vy, sems_vy, NY), vz, sems_vz, NZ, at_z)

    for t in range(4):
        for j in range(1, NZ):
            there = z_all.at[(mz + NZ - j) % NZ, t]
            copy(there, there, l_send.at[t, j], l_recv.at[t, j], mate).wait_recv()
    total = (z_all[0] + z_all[1]) + (z_all[2] + z_all[3])
    flat = total.reshape(32, 128)
    upper = dot(flat, green_one[:128, :], NN, HIGHEST)
    lower = dot(flat, green_one[128:, :], NN, HIGHEST)
    done = []
    for t in range(4):
        both = upper[8 * t : 8 * t + 8] + pltpu.roll(lower[8 * t : 8 * t + 8], 4, 0)
        done.append(both * scales[t])
    top2 = iota((8, 256), 0) < 4
    first = jnp.where(top2, done[0], pltpu.roll(done[1], 4, 0))
    second = jnp.where(top2, done[2], pltpu.roll(done[3], 4, 0))
    dressed[mx, my] = jnp.concatenate([first, second], axis=0).astype(BF16)

    def along_x(j):
        here = dressed.at[mx, (my + NY - j) % NY]
        for i in (2, 1, 3):
            send(here, here, gx_send.at[j, i], gx_recv.at[j, i], at_x(i))

    order = (1, 7, 2, 6, 3, 5, 4)
    here = dressed.at[mx, my]
    for j in order[::-1]:
        send(here, here, gy_send.at[j], gy_recv.at[j], at_y(j))
    along_x(0)
    vec[...] = collect(vz, sems_vz, NZ)
    traced = jnp.zeros((1, 512), F32)
    for t in range(4):
        traced = traced + exact(vec[t : t + 1, :] * weights[t], chol_t[t].reshape(128, 512), NN)
    for a in range(2 * NH):
        @pl.when(aux == a)
        def _():
            collision[...] = traced[:, 64 * a : 64 * a + 64]

    for j in order:
        there = dressed.at[mx, (my + NY - j) % NY]
        copy(there, there, gy_send.at[j], gy_recv.at[j], mate).wait_recv()
        along_x(j)

    for i in range(1, NX):
        for j in range(NY):
            there = dressed.at[(mx + NX - i) % NX, (my + NY - j) % NY]
            copy(there, there, gx_send.at[j, i], gx_recv.at[j, i], mate).wait_recv()

    for made, when in sent:
        if when is None:
            made.wait_send()
        else:
            pl.when(when)(made.wait_send)


SEMS = (
    (4,), (), (), (4, CHUNKS), (4, CHUNKS), (4, CHUNKS), (4, CHUNKS), (4, CHUNKS), None, (), (), (8,), (4,), None, 2, 2,
    (4, NX), (4, NX), (4, NY), (4, NY), (4, NZ), (4, NZ), (NY,), (NY,), (NY, NX), (NY, NX),
    (NX,), (NX,), (NY,), (NY,), (NZ,), (NZ,),
)


def semaphores(shape):
    if shape is None:
        return pltpu.SemaphoreType.REGULAR
    if isinstance(shape, int):
        return pltpu.SemaphoreType.REGULAR((shape,))
    return pltpu.SemaphoreType.DMA(shape)


def local(pair_green_block, cholesky_factors, green_one, screening):
    vmem = pltpu.VMEM
    tile = (8, 128)
    chol_p, dressed, collision = pl.pallas_call(
        gather_kernel,
        out_shape=(
            pltpu.VMEM((512, 512), BF16),
            pltpu.VMEM((NX, NY, 16, 256), BF16),
            pltpu.VMEM((1, 64), F32),
        ),
        in_specs=[pl.BlockSpec(memory_space=pl.ANY)] * 4,
        out_specs=(pl.BlockSpec(memory_space=vmem),) * 3,
        scratch_shapes=[
            vmem((512, 256), BF16), vmem((256, 256), F32), vmem((4, 128), F32),
            vmem((4, 2, 64, 512), BF16),
            vmem((4, NX, NY) + tile, F32),
            vmem((4, NX, NY) + tile, F32),
            vmem((4, NY) + tile, F32),
            vmem((4, NY) + tile, F32),
            vmem((NZ, 4) + tile, F32),
            vmem(tile, F32),
            vmem((NX,) + tile, F32), vmem((NY,) + tile, F32), vmem((NZ,) + tile, F32), vmem((4,) + tile, F32), vmem((2,) + tile, F32),
        ] + [semaphores(shape) for shape in SEMS],
        compiler_params=pltpu.CompilerParams(collective_id=0, has_side_effects=True),
    )(pair_green_block, cholesky_factors.T, green_one, screening.reshape(4, 128))
    slope = jnp.dot(chol_p, dressed.reshape(512, 256), preferred_element_type=F32)
    return slope, collision.reshape(64)


def solution(mesh):
    placed = (P("rows", "aux"), P("rows", "aux"), P(), P())
    return jax.shard_map(
        local,
        mesh=mesh,
        in_specs=placed,
        out_specs=(P("rows", "aux"), P(("rows", "aux"))),
        check_vma=False,
    )
```
